32 devices in a mesh: group: 2 (over y), section: 4 (over z), tensor: 4 (over x, core).
Axes of the slice: x: 2, y: 2, z: 4, core: 2. Of those that a mesh axis runs over, the one named last changes fastest.
Arguments:
- inputs: bfloat16 [48, 4096], P('group', 'tensor'), parts along dimension 0, may hold values from -6 to 6
- gains: float32 [4, 4096], P('section'), may hold values from 0.5 to 1.5
- w_query: bfloat16 [4, 4096, 4096], P('section', None, 'tensor'), may hold values from -0.09375 to 0.09375
- w_key: bfloat16 [4, 4096, 1024], P('section', None, 'tensor'), may hold values from -0.09375 to 0.09375
- w_value: bfloat16 [4, 4096, 1024], P('section', None, 'tensor'), may hold values from -0.09375 to 0.09375
- w_out: bfloat16 [4, 4096, 4096], P('section', 'tensor'), may hold values from -0.375 to 0.375
- key_cache: bfloat16 [4, 48, 128, 1024], P('section', 'group', None, 'tensor'), parts along dimension 1, may hold values from -64 to 64
- value_cache: bfloat16 [4, 48, 128, 1024], P('section', 'group', None, 'tensor'), parts along dimension 1, may hold values from -6 to 6
- cache_lens: int32 [48], P('group'), parts along dimension 0, may hold values from 1 to 128, as said below
- exit_plan: int32 [48], P('group'), parts along dimension 0, may hold values from 1 to 4, as said below
Outputs:
- section_hidden: bfloat16 [4, 48, 4096], P('section', 'group', 'tensor'), parts along dimension 1
- new_keys: bfloat16 [4, 48, 1024], P('section', 'group', 'tensor'), parts along dimension 1
- new_values: bfloat16 [4, 48, 1024], P('section', 'group', 'tensor'), parts along dimension 1
The draws below stay inside these ranges and needn't reach their ends.
There are 2 independent parts, one for each index of `group`. The reference program is written for one: setup_inputs(seed, part) draws one part's arguments, and reference() takes and returns one part's arrays. A program takes and returns all parts, laid end to end along the dimension named above; an argument that names none is the same for every part. Nothing has to cross between parts.
Inputs may be any that keep to these rules, and one draw needn't show every extreme that they name: Cached slots 0 to cache_lens - 1 of a row are live; some row has exactly 128. `exit_plan`: some row runs all 4 layers in full.
All inputs are finite; a program needn't handle non-finite values.
Results may differ from the reference program's by a relative error of at most 0.022.
The reference program's roundings to bfloat16 on the way count: a program that leaves them out, or rounds other values in their place, can miss the bound.
Values may be sent and summed in bfloat16 or wider, within the bound.
A program may use at most 128 MiB of HBM per device.

```python
import math
import jax
import jax.numpy as jnp
from jax import lax

D = 4096
HEADS = 32
KV_HEADS = 8
HEAD_DIM = 128
ROWS = 24
CACHE_LEN = 128
LAYERS = 4


def draw_key_cache(key, part):
    standard = jnp.clip(jax.random.normal(jax.random.fold_in(key, 11), (LAYERS, ROWS, CACHE_LEN, KV_HEADS * HEAD_DIM), jnp.float32), -4.0, 4.0)
    return standard.astype(jnp.bfloat16)


def draw_cache_lens(key, part):
    lengths = jax.random.randint(jax.random.fold_in(key, 21), (ROWS,), 1, CACHE_LEN + 1)
    chosen = jax.random.randint(jax.random.fold_in(key, 22), (), 0, ROWS)
    return lengths.at[chosen].set(CACHE_LEN).astype(jnp.int32)


def draw_exit_plan(key, part):
    planned = jax.random.randint(jax.random.fold_in(key, 31), (ROWS,), 1, LAYERS + 1)
    chosen = jax.random.randint(jax.random.fold_in(key, 32), (), 0, ROWS)
    return planned.at[chosen].set(LAYERS).astype(jnp.int32)


def block_scale(key, extent, cuts, least, high):
    gain = 1.0
    for dim, blocks in cuts:
        steps = jax.random.uniform(jax.random.fold_in(jax.random.fold_in(key, 6), dim), (blocks,), jnp.float32, least / len(cuts), high / len(cuts))
        gain = gain * jnp.repeat(jnp.exp(steps), extent[dim] // blocks).reshape((-1,) + (1,) * (len(extent) - 1 - dim))
    return gain


def centred(stream_key, dims, scale, bound, split=(), kind=jnp.bfloat16):
    drawn = scale * jax.random.normal(stream_key, dims, jnp.float32)
    if split:
        drawn = drawn * block_scale(stream_key, dims, split, -0.22, 0.18)
    return jnp.clip(drawn, -bound, bound).astype(kind)


def setup_inputs(seed: int = 0, part: int = 0) -> dict:
    key_of = jax.random.split(jax.random.key(seed), 11)
    own_keys = jax.random.split(jax.random.fold_in(key_of[10], part), 11)
    inputs = centred(own_keys[0], (ROWS, D), 1.0, 6.0, ((1, 4),))
    gains = jnp.clip(1.0 + 0.1 * jax.random.normal(key_of[1], (LAYERS, D), jnp.float32), 0.5, 1.5)
    w_query = centred(key_of[2], (LAYERS, D, HEADS * HEAD_DIM), D ** -0.5, 0.09375, ((0, 4), (2, 4)))
    w_key = centred(key_of[3], (LAYERS, D, KV_HEADS * HEAD_DIM), D ** -0.5, 0.09375, ((0, 4), (2, 4)))
    w_value = centred(key_of[4], (LAYERS, D, KV_HEADS * HEAD_DIM), D ** -0.5, 0.09375, ((0, 4), (2, 4)))
    w_out = centred(key_of[5], (LAYERS, HEADS * HEAD_DIM, D), (HEADS * HEAD_DIM // 16) ** -0.5, 0.375, ((0, 4), (1, 4)))
    key_cache = draw_key_cache(jax.random.fold_in(jax.random.fold_in(key_of[10], part), 71), part)
    value_cache = centred(own_keys[7], (LAYERS, ROWS, CACHE_LEN, KV_HEADS * HEAD_DIM), 1.0, 6.0, ((0, 4), (3, 4)))
    cache_lens = draw_cache_lens(jax.random.fold_in(jax.random.fold_in(key_of[10], part), 71), part)
    exit_plan = draw_exit_plan(jax.random.fold_in(jax.random.fold_in(key_of[10], part), 71), part)
    return dict(inputs=inputs, gains=gains, w_query=w_query, w_key=w_key, w_value=w_value, w_out=w_out, key_cache=key_cache, value_cache=value_cache, cache_lens=cache_lens, exit_plan=exit_plan)


NORM_EPSILON = 1e-05
ROPE_BASE = 500000.0
MASKED_SCORE = -1e+30

def rotate(vectors, positions):
    half_dim = vectors.shape[-1] // 2
    frequency = ROPE_BASE ** (-(jnp.arange(half_dim, dtype=jnp.float32) * 2.0 / vectors.shape[-1]))
    angles = positions.astype(jnp.float32)[:, None, None] * frequency[None, None, :]
    cos_part = jnp.cos(angles)
    sin_part = jnp.sin(angles)
    lower_half = vectors[..., :half_dim]
    upper_half = vectors[..., half_dim:]
    return jnp.concatenate([lower_half * cos_part - upper_half * sin_part, upper_half * cos_part + lower_half * sin_part], axis=-1)

def reference(inputs, gains, w_query, w_key, w_value, w_out, key_cache, value_cache, cache_lens, exit_plan):
    per_kv = HEADS // KV_HEADS
    inv_root = 1.0 / math.sqrt(HEAD_DIM)
    visible = jnp.arange(CACHE_LEN)[None, :] < cache_lens[:, None]
    hidden = inputs
    hidden_list = []
    key_list = []
    value_list = []
    for depth_at in range(LAYERS):
        widened = hidden.astype(jnp.float32)
        normed = (widened * lax.rsqrt(lax.optimization_barrier(jnp.mean(widened * widened, axis=-1, keepdims=True)) + NORM_EPSILON) * gains[depth_at][None, :]).astype(jnp.bfloat16)
        queries = jnp.dot(normed, w_query[depth_at], preferred_element_type=jnp.float32).reshape(ROWS, HEADS, HEAD_DIM)
        queries = rotate(queries, cache_lens).astype(jnp.bfloat16).reshape(ROWS, KV_HEADS, per_kv, HEAD_DIM)
        key_new = jnp.dot(normed, w_key[depth_at], preferred_element_type=jnp.float32).reshape(ROWS, KV_HEADS, HEAD_DIM)
        key_new = rotate(key_new, cache_lens).astype(jnp.bfloat16)
        value_new = jnp.dot(normed, w_value[depth_at], preferred_element_type=jnp.float32).astype(jnp.bfloat16).reshape(ROWS, KV_HEADS, HEAD_DIM)
        keys_old = key_cache[depth_at].reshape(ROWS, CACHE_LEN, KV_HEADS, HEAD_DIM).astype(jnp.float32)
        values_old = value_cache[depth_at].reshape(ROWS, CACHE_LEN, KV_HEADS, HEAD_DIM).astype(jnp.float32)
        query_wide = queries.astype(jnp.float32)
        scores_old = jnp.einsum('rhgd,rlhd->rhgl', query_wide, keys_old) * inv_root
        scores_old = jnp.where(visible[:, None, None, :], scores_old, MASKED_SCORE)
        score_new = jnp.einsum('rhgd,rhd->rhg', query_wide, key_new.astype(jnp.float32)) * inv_root
        highest = jnp.maximum(lax.optimization_barrier(jnp.max(scores_old, axis=-1)), score_new)
        weight_old = jnp.exp(scores_old - highest[..., None])
        weight_new = jnp.exp(score_new - highest)
        denominator = lax.optimization_barrier(jnp.sum(weight_old, axis=-1)) + weight_new
        weight_old = (weight_old / denominator[..., None]).astype(jnp.bfloat16)
        weight_new = (weight_new / denominator).astype(jnp.bfloat16)
        attended = jnp.einsum('rhgl,rlhd->rhgd', weight_old.astype(jnp.float32), values_old)
        attended = attended + weight_new.astype(jnp.float32)[..., None] * value_new.astype(jnp.float32)[:, :, None, :]
        attended = attended.astype(jnp.bfloat16).reshape(ROWS, HEADS * HEAD_DIM)
        update = jnp.dot(attended, w_out[depth_at], preferred_element_type=jnp.float32)
        running = (depth_at < exit_plan).astype(jnp.float32)[:, None]
        hidden = (widened + running * update).astype(jnp.bfloat16)
        hidden_list.append(hidden)
        key_list.append(key_new.reshape(ROWS, KV_HEADS * HEAD_DIM))
        value_list.append(value_new.reshape(ROWS, KV_HEADS * HEAD_DIM))
    return (jnp.stack(hidden_list), jnp.stack(key_list), jnp.stack(value_list))
```

```python
import functools
import math

import jax
import jax.numpy as jnp
from jax import lax
from jax.experimental import pallas as pl
from jax.experimental.pallas import tpu as pltpu
from jax.sharding import PartitionSpec as P

HEAD_DIM = 128
NORM_EPSILON = 1e-05
ROPE_BASE = 500000.0
MASKED_SCORE = -1e30
MESH = pl.DeviceIdType.MESH


def relay_kernel(
    sections, tensors, groups_per_kv,
    lens_ref, plan_ref, inputs_ref, gains_ref, wq_ref, wk_ref, wv_ref, wo_ref, kc_ref, vc_ref,
    out_hidden, out_keys, out_values,
    wq, wk, wv, wo, kc, vc, gain, hid, part, arrived, piece, normed,
    pos, running, mask, queries, scores, score_new, values_new, attended,
    load_sem, hid_send, hid_recv, part_send, part_recv,
):
    rows, width = hid.shape[1], hid.shape[2]
    kv_local = wk.shape[1] // HEAD_DIM
    heads = kv_local * groups_per_kv
    slot = queries.shape[0] // rows
    slots = kc.shape[1]
    section = lax.axis_index("section")
    me = lax.axis_index("tensor")

    def load(source, target, index):
        return pltpu.make_async_copy(source, target, load_sem.at[index])

    loads = dict(
        gain=load(gains_ref, gain, 0),
        wk=load(wk_ref.at[0], wk, 1),
        wv=load(wv_ref.at[0], wv, 2),
        wq=load(wq_ref.at[0], wq, 3),
        kc=load(kc_ref.at[0], kc, 4),
        vc=load(vc_ref.at[0], vc, 5),
        wo=load(wo_ref.at[0], wo, 6),
    )
    own_entering = pltpu.make_async_copy(inputs_ref, hid.at[me], load_sem.at[7])
    for name in ("gain", "wk", "wv", "wq"):
        loads[name].start()

    @pl.when(section == 0)
    def _():
        own_entering.start()

    for name in ("kc", "vc", "wo"):
        loads[name].start()

    barrier = pltpu.get_barrier_semaphore()
    for off in range(1, tensors):
        pl.semaphore_signal(
            barrier, inc=1, device_id={"tensor": lax.rem(me + off, tensors)}, device_id_type=MESH
        )

    @pl.when(section > 0)
    def _():
        for other in range(tensors):
            pl.semaphore_signal(
                barrier, inc=1,
                device_id={"section": section - 1, "tensor": jnp.int32(other)}, device_id_type=MESH,
            )

    @pl.when(section < sections - 1)
    def _():
        for other in range(tensors):
            pl.semaphore_signal(
                barrier, inc=1,
                device_id={"section": section + 1, "tensor": jnp.int32(other)}, device_id_type=MESH,
            )

    lane = lax.broadcasted_iota(jnp.int32, (slot, slots), 1)
    for row in range(rows):
        length = lens_ref[row]
        pos[row : row + 1, :] = jnp.full((1, HEAD_DIM), length, jnp.int32).astype(jnp.float32)
        runs = jnp.full((1, HEAD_DIM), plan_ref[row], jnp.int32) > section
        running[row : row + 1, :] = runs.astype(jnp.float32)
        mask[row * slot : (row + 1) * slot, :] = (lane < length).astype(jnp.float32)
    half_lane = lax.broadcasted_iota(jnp.int32, (rows, HEAD_DIM), 1)
    half = HEAD_DIM // 2
    step_at = jnp.where(half_lane < half, half_lane, half_lane - half).astype(jnp.float32)
    frequency = jnp.exp(step_at * (-2.0 * math.log(ROPE_BASE) / HEAD_DIM))
    angles = pos[...] * frequency
    cos_part = jnp.cos(angles)
    sin_part = jnp.sin(angles)
    sin_part = jnp.where(half_lane < half, -sin_part, sin_part)

    def rotate(vectors):
        return vectors * cos_part + pltpu.roll(vectors, half, 1) * sin_part

    pl.semaphore_wait(
        barrier,
        (tensors - 1)
        + tensors * (section > 0).astype(jnp.int32)
        + tensors * (section < sections - 1).astype(jnp.int32),
    )

    def entering(off):
        return pltpu.make_async_remote_copy(
            src_ref=inputs_ref,
            dst_ref=hid.at[me],
            send_sem=hid_send.at[off],
            recv_sem=hid_recv.at[me],
            device_id={"tensor": lax.rem(me + off, tensors)},
            device_id_type=MESH,
        )

    def await_hidden(source):
        pltpu.make_async_remote_copy(
            src_ref=hid.at[source],
            dst_ref=hid.at[source],
            send_sem=hid_send.at[0],
            recv_sem=hid_recv.at[source],
            device_id={"tensor": lax.rem(me + 1, tensors)},
            device_id_type=MESH,
        ).wait_recv()

    @pl.when(section == 0)
    def _():
        for off in range(1, tensors):
            entering(off).start()
        own_entering.wait()
        for off in range(1, tensors):
            await_hidden(lax.rem(me + off, tensors))
        for off in range(1, tensors):
            entering(off).wait_send()

    @pl.when(section > 0)
    def _():
        for source in range(tensors):
            await_hidden(source)

    loads["gain"].wait()
    squares = jnp.zeros((rows, 1), jnp.float32)
    for source in range(tensors):
        wide = hid[source].astype(jnp.float32)
        squares = squares + jnp.sum(wide * wide, axis=-1, keepdims=True)
    scale = lax.rsqrt(squares / (tensors * width) + NORM_EPSILON)
    for source in range(tensors):
        at = slice(source * width, (source + 1) * width)
        normed[:, at] = (hid[source].astype(jnp.float32) * scale * gain[:, at]).astype(jnp.bfloat16)

    entered = normed[...]
    loads["wk"].wait()
    key_new = jnp.dot(entered, wk[...], preferred_element_type=jnp.float32)
    loads["wv"].wait()
    value_new = jnp.dot(entered, wv[...], preferred_element_type=jnp.float32).astype(jnp.bfloat16)
    out_values[0] = value_new
    keys = []
    values = []
    for kv in range(kv_local):
        at = slice(kv * HEAD_DIM, (kv + 1) * HEAD_DIM)
        rotated = rotate(key_new[:, at]).astype(jnp.bfloat16)
        out_keys[0, :, at] = rotated
        keys.append(rotated.astype(jnp.float32))
        values.append(value_new[:, at].astype(jnp.float32))

    loads["wq"].wait()
    inv_root = 1.0 / math.sqrt(HEAD_DIM)
    if heads < slot:
        queries[...] = jnp.zeros_like(queries)
        score_new[...] = jnp.zeros_like(score_new)
        values_new[...] = jnp.zeros_like(values_new)
    tile = min(256, heads * HEAD_DIM)
    for start in range(0, heads * HEAD_DIM, tile):
        product = jnp.dot(
            entered, wq[:, start : start + tile], preferred_element_type=jnp.float32
        )
        for inner in range(tile // HEAD_DIM):
            head = start // HEAD_DIM + inner
            kv = head // groups_per_kv
            query = rotate(product[:, inner * HEAD_DIM : (inner + 1) * HEAD_DIM])
            query = query.astype(jnp.bfloat16).astype(jnp.float32)
            at = pl.ds(head, rows, stride=slot)
            queries[at, :] = query
            score = jnp.sum(query * keys[kv], axis=-1, keepdims=True) * inv_root
            score_new[at, :] = jnp.broadcast_to(score, (rows, HEAD_DIM))
            values_new[at, :] = values[kv]

    loads["kc"].wait()
    head_of = lax.broadcasted_iota(jnp.int32, (slot, HEAD_DIM), 0) // groups_per_kv
    for row in range(rows):
        at = slice(row * slot, (row + 1) * slot)
        query = queries[at, :]
        spread = jnp.concatenate(
            [jnp.where(head_of == kv, query, 0.0) for kv in range(kv_local)], axis=1
        ).astype(jnp.bfloat16)
        scores[at, :] = lax.dot_general(
            spread, kc[row], (((1,), (1,)), ((), ())), preferred_element_type=jnp.float32
        )

    old = jnp.where(mask[...] > 0.0, scores[...] * inv_root, MASKED_SCORE)
    new = score_new[:, :1]
    highest = jnp.maximum(jnp.max(old, axis=-1, keepdims=True), new)
    weight_old = jnp.exp(old - highest)
    weight_new = jnp.exp(new - highest)
    denominator = jnp.sum(weight_old, axis=-1, keepdims=True) + weight_new
    scores[...] = weight_old / denominator
    weight_new = (weight_new / denominator).astype(jnp.bfloat16).astype(jnp.float32)
    values_new[...] = values_new[...] * weight_new

    loads["vc"].wait()
    for row in range(rows):
        at = slice(row * slot, (row + 1) * slot)
        mixed = jnp.dot(
            scores[at, :].astype(jnp.bfloat16), vc[row], preferred_element_type=jnp.float32
        )
        taken = mixed[:, :HEAD_DIM]
        for kv in range(1, kv_local):
            taken = jnp.where(head_of == kv, mixed[:, kv * HEAD_DIM : (kv + 1) * HEAD_DIM], taken)
        attended[at, :] = taken + values_new[at, :]

    flat = jnp.concatenate(
        [
            attended[pl.ds(head, rows, stride=slot), :].astype(jnp.bfloat16)
            for head in range(heads)
        ],
        axis=1,
    )

    loads["wo"].wait()

    def send_part(off):
        peer = lax.rem(me + off, tensors)
        return pltpu.make_async_remote_copy(
            src_ref=part.at[off],
            dst_ref=arrived.at[off],
            send_sem=part_send.at[off],
            recv_sem=part_recv.at[off],
            device_id={"tensor": peer},
            device_id_type=MESH,
        )

    def project(target):
        columns = pl.ds(pl.multiple_of(target * width, width), width)
        return jnp.dot(flat, wo[:, columns], preferred_element_type=jnp.float32)

    order = sorted(range(1, tensors), key=lambda off: -min(off, tensors - off))
    for off in order:
        part[off] = project(lax.rem(me + off, tensors)).astype(jnp.bfloat16)
        send_part(off).start()
    total = project(me)
    for off in range(1, tensors):
        send_part(off).wait_recv()
        total = total + arrived[off].astype(jnp.float32)
    following = (hid[me].astype(jnp.float32) + running[:, :1] * total).astype(jnp.bfloat16)
    piece[...] = following

    def pass_on(other):
        return pltpu.make_async_remote_copy(
            src_ref=piece,
            dst_ref=hid.at[me],
            send_sem=hid_send.at[other],
            recv_sem=hid_recv.at[me],
            device_id={"section": section + 1, "tensor": lax.rem(me + other, tensors)},
            device_id_type=MESH,
        )

    @pl.when(section < sections - 1)
    def _():
        for other in range(tensors):
            pass_on(other).start()

    out_hidden[0] = following
    for off in range(1, tensors):
        send_part(off).wait_send()

    @pl.when(section < sections - 1)
    def _():
        for other in range(tensors):
            pass_on(other).wait_send()


def solution(mesh):
    sections = mesh.shape["section"]
    tensors = mesh.shape["tensor"]

    def per_device(
        inputs, gains, w_query, w_key, w_value, w_out, key_cache, value_cache, cache_lens, exit_plan
    ):
        rows, width = inputs.shape
        features = gains.shape[1]
        query_width = w_query.shape[2]
        kv_width = w_key.shape[2]
        heads = query_width // HEAD_DIM
        groups_per_kv = query_width // kv_width
        slot = -(-heads // 8) * 8
        slots = key_cache.shape[2]
        any_spec = pl.BlockSpec(memory_space=pl.ANY)
        smem_spec = pl.BlockSpec(memory_space=pltpu.SMEM)
        vmem_spec = pl.BlockSpec(memory_space=pltpu.VMEM)
        bf16, f32 = jnp.bfloat16, jnp.float32
        return pl.pallas_call(
            functools.partial(relay_kernel, sections, tensors, groups_per_kv),
            out_shape=(
                jax.ShapeDtypeStruct((1, rows, width), bf16),
                jax.ShapeDtypeStruct((1, rows, kv_width), bf16),
                jax.ShapeDtypeStruct((1, rows, kv_width), bf16),
            ),
            in_specs=[smem_spec] * 2 + [any_spec] * 8,
            out_specs=(vmem_spec,) * 3,
            scratch_shapes=[
                pltpu.VMEM((features, query_width), bf16),
                pltpu.VMEM((features, kv_width), bf16),
                pltpu.VMEM((features, kv_width), bf16),
                pltpu.VMEM((query_width, features), bf16),
                pltpu.VMEM((rows, slots, kv_width), bf16),
                pltpu.VMEM((rows, slots, kv_width), bf16),
                pltpu.VMEM((1, features), f32),
                pltpu.VMEM((tensors, rows, width), bf16),
                pltpu.VMEM((tensors, rows, width), bf16),
                pltpu.VMEM((tensors, rows, width), bf16),
                pltpu.VMEM((rows, width), bf16),
                pltpu.VMEM((rows, features), bf16),
                pltpu.VMEM((rows, HEAD_DIM), f32),
                pltpu.VMEM((rows, HEAD_DIM), f32),
                pltpu.VMEM((rows * slot, slots), f32),
                pltpu.VMEM((rows * slot, HEAD_DIM), f32),
                pltpu.VMEM((rows * slot, slots), f32),
                pltpu.VMEM((rows * slot, HEAD_DIM), f32),
                pltpu.VMEM((rows * slot, HEAD_DIM), f32),
                pltpu.VMEM((rows * slot, HEAD_DIM), f32),
                pltpu.SemaphoreType.DMA((8,)),
                pltpu.SemaphoreType.DMA((tensors,)),
                pltpu.SemaphoreType.DMA((tensors,)),
                pltpu.SemaphoreType.DMA((tensors,)),
                pltpu.SemaphoreType.DMA((tensors,)),
            ],
            compiler_params=pltpu.CompilerParams(
                collective_id=0, has_side_effects=True, vmem_limit_bytes=48 * 1024 * 1024
            ),
            name="relay",
        )(
            cache_lens, exit_plan, inputs, gains, w_query, w_key, w_value, w_out,
            key_cache, value_cache,
        )

    return jax.shard_map(
        per_device,
        mesh=mesh,
        in_specs=(
            P("group", "tensor"),
            P("section", None),
            P("section", None, "tensor"),
            P("section", None, "tensor"),
            P("section", None, "tensor"),
            P("section", "tensor", None),
            P("section", "group", None, "tensor"),
            P("section", "group", None, "tensor"),
            P("group"),
            P("group"),
        ),
        out_specs=(
            P("section", "group", "tensor"),
            P("section", "group", "tensor"),
            P("section", "group", "tensor"),
        ),
        check_vma=False,
    )
```

```python
import functools
import math

import jax
import jax.numpy as jnp
from jax import lax
from jax.experimental import pallas as pl
from jax.experimental.pallas import tpu as pltpu
from jax.sharding import PartitionSpec as P

HEAD_DIM = 128
NORM_EPSILON = 1e-05
ROPE_BASE = 500000.0
MASKED_SCORE = -1e30
MESH = pl.DeviceIdType.MESH


def relay_kernel(
    sections, tensors, groups_per_kv,
    lens_ref, plan_ref, inputs_ref, gains_ref, wq_ref, wk_ref, wv_ref, wo_ref, kc_ref, vc_ref,
    out_hidden, out_keys, out_values,
    wq, wk, wv, wo, kc, vc, gain, hid, before, part, part_in, chip_sum, sums_in, piece_in, normed,
    pos, running, mask, queries, scores, score_new, values_new, attended,
    load_sem, enter_send, enter_recv, half_send, half_recv, before_send, before_recv,
    part_send, part_recv, sums_send, sums_recv, piece_send, piece_recv,
):
    rows, width = hid.shape[2], hid.shape[3]
    chips = tensors // 2
    kv_local = wk.shape[1] // HEAD_DIM
    heads = kv_local * groups_per_kv
    slot = queries.shape[0] // rows
    slots = kc.shape[1]
    section = lax.axis_index("section")
    me = lax.axis_index("tensor")
    chip = me // 2
    core = lax.rem(me, 2)
    sibling = {"tensor": 2 * chip + 1 - core}

    def load(source, target, index):
        return pltpu.make_async_copy(source, target, load_sem.at[index])

    def remote(source, target, send_sem, recv_sem, device):
        return pltpu.make_async_remote_copy(
            src_ref=source, dst_ref=target, send_sem=send_sem, recv_sem=recv_sem,
            device_id=device, device_id_type=MESH,
        )

    loads = dict(
        gain=load(gains_ref, gain, 0),
        wk=load(wk_ref.at[0], wk, 1),
        wv=load(wv_ref.at[0], wv, 2),
        wq=load(wq_ref.at[0], wq, 3),
        kc=load(kc_ref.at[0], kc, 4),
        vc=load(vc_ref.at[0], vc, 5),
        wo=load(wo_ref.at[0], wo, 6),
    )
    own_entering = pltpu.make_async_copy(inputs_ref, hid.at[core, chip], load_sem.at[7])

    @pl.when(section == 0)
    def _():
        own_entering.start()

    for name in ("gain", "wk", "wv", "wq", "kc"):
        loads[name].start()

    @pl.when(section > 0)
    def _():
        for name in ("vc", "wo"):
            loads[name].start()

    barrier = pltpu.get_barrier_semaphore()

    def greet(device):
        pl.semaphore_signal(barrier, inc=1, device_id=device, device_id_type=MESH)

    for off in range(1, tensors):
        greet({"tensor": lax.rem(me + off, tensors)})

    @pl.when(section > 0)
    def _():
        for other in range(chips):
            greet({"section": section - 1, "tensor": 2 * other + core})

    @pl.when(section < sections - 1)
    def _():
        for other in range(chips):
            greet({"section": section + 1, "tensor": 2 * other + core})

    lane = lax.broadcasted_iota(jnp.int32, (slot, slots), 1)
    for row in range(rows):
        length = lens_ref[row]
        pos[row : row + 1, :] = jnp.full((1, HEAD_DIM), length, jnp.int32).astype(jnp.float32)
        planned = jnp.full((1, HEAD_DIM), plan_ref[row], jnp.int32)
        running[0, row : row + 1, :] = (planned > section).astype(jnp.float32)
        running[1, row : row + 1, :] = (planned > section - 1).astype(jnp.float32)
        mask[row * slot : (row + 1) * slot, :] = (lane < length).astype(jnp.float32)
    half_lane = lax.broadcasted_iota(jnp.int32, (rows, HEAD_DIM), 1)
    half = HEAD_DIM // 2
    step_at = jnp.where(half_lane < half, half_lane, half_lane - half).astype(jnp.float32)
    frequency = jnp.exp(step_at * (-2.0 * math.log(ROPE_BASE) / HEAD_DIM))
    angles = pos[...] * frequency
    cos_part = jnp.cos(angles)
    sin_part = jnp.sin(angles)
    sin_part = jnp.where(half_lane < half, -sin_part, sin_part)

    def rotate(vectors):
        return vectors * cos_part + pltpu.roll(vectors, half, 1) * sin_part

    pl.semaphore_wait(
        barrier,
        (tensors - 1)
        + chips * (section > 0).astype(jnp.int32)
        + chips * (section < sections - 1).astype(jnp.int32),
    )

    def entering(off):
        return remote(
            inputs_ref, hid.at[core, chip], enter_send.at[off], enter_recv.at[core, chip],
            {"tensor": lax.rem(me + off, tensors)},
        )

    def swap_half(half, at):
        return remote(
            hid.at[half, at], hid.at[half, at], half_send.at[at], half_recv.at[at], sibling
        )

    def send_sum(target, at):
        return remote(
            chip_sum.at[at], sums_in.at[chip, at], sums_send.at[target, at],
            sums_recv.at[chip, at], {"section": section + 1, "tensor": 2 * target + core},
        )

    def send_before():
        return remote(
            hid.at[core], before, before_send.at[0], before_recv.at[0], {"section": section + 1}
        )

    @pl.when(section == 0)
    def _():
        for off in range(1, tensors):
            entering(off).start()
        own_entering.wait()
        for off in range(1, tensors):
            other = lax.rem(me + off, tensors)
            at = (lax.rem(other, 2), other // 2)
            remote(
                hid.at[at], hid.at[at], enter_send.at[off], enter_recv.at[at], sibling
            ).wait_recv()
        for name in ("vc", "wo"):
            loads[name].start()
        for off in range(1, tensors):
            entering(off).wait_send()

    @pl.when(section > 0)
    def _():
        remote(
            before, before, before_send.at[0], before_recv.at[0], {"section": section - 1}
        ).wait_recv()
        for at in range(chips):
            total = jnp.zeros((rows, width), jnp.float32)
            for source in range(chips):
                remote(
                    sums_in.at[source, at], sums_in.at[source, at], sums_send.at[source, at],
                    sums_recv.at[source, at], {"section": section - 1},
                ).wait_recv()
                total = total + sums_in[source, at].astype(jnp.float32)
            wide = before[at].astype(jnp.float32)
            hid[core, at] = (wide + running[1, :, :1] * total).astype(jnp.bfloat16)
            swap_half(core, at).start()
        for at in range(chips):
            swap_half(1 - core, at).wait_recv()

    @pl.when(section < sections - 1)
    def _():
        send_before().start()

    loads["gain"].wait()
    squares = jnp.zeros((rows, 1), jnp.float32)
    for source in range(tensors):
        wide = hid[source % 2, source // 2].astype(jnp.float32)
        squares = squares + jnp.sum(wide * wide, axis=-1, keepdims=True)
    scale = lax.rsqrt(squares / (tensors * width) + NORM_EPSILON)
    for source in range(tensors):
        at = slice(source * width, (source + 1) * width)
        wide = hid[source % 2, source // 2].astype(jnp.float32)
        normed[:, at] = (wide * scale * gain[:, at]).astype(jnp.bfloat16)

    entered = normed[...]
    loads["wk"].wait()
    key_new = jnp.dot(entered, wk[...], preferred_element_type=jnp.float32)
    loads["wv"].wait()
    value_new = jnp.dot(entered, wv[...], preferred_element_type=jnp.float32).astype(jnp.bfloat16)
    out_values[0] = value_new
    keys = []
    values = []
    for kv in range(kv_local):
        at = slice(kv * HEAD_DIM, (kv + 1) * HEAD_DIM)
        rotated = rotate(key_new[:, at]).astype(jnp.bfloat16)
        out_keys[0, :, at] = rotated
        keys.append(rotated.astype(jnp.float32))
        values.append(value_new[:, at].astype(jnp.float32))

    loads["wq"].wait()
    inv_root = 1.0 / math.sqrt(HEAD_DIM)
    if heads < slot:
        queries[...] = jnp.zeros_like(queries)
        score_new[...] = jnp.zeros_like(score_new)
        values_new[...] = jnp.zeros_like(values_new)
    tile = min(256, heads * HEAD_DIM)
    for start in range(0, heads * HEAD_DIM, tile):
        product = jnp.dot(
            entered, wq[:, start : start + tile], preferred_element_type=jnp.float32
        )
        for inner in range(tile // HEAD_DIM):
            head = start // HEAD_DIM + inner
            kv = head // groups_per_kv
            query = rotate(product[:, inner * HEAD_DIM : (inner + 1) * HEAD_DIM])
            query = query.astype(jnp.bfloat16).astype(jnp.float32)
            at = pl.ds(head, rows, stride=slot)
            queries[at, :] = query
            score = jnp.sum(query * keys[kv], axis=-1, keepdims=True) * inv_root
            score_new[at, :] = jnp.broadcast_to(score, (rows, HEAD_DIM))
            values_new[at, :] = values[kv]

    loads["kc"].wait()
    head_of = lax.broadcasted_iota(jnp.int32, (slot, HEAD_DIM), 0) // groups_per_kv
    for row in range(rows):
        at = slice(row * slot, (row + 1) * slot)
        query = queries[at, :]
        spread = jnp.concatenate(
            [jnp.where(head_of == kv, query, 0.0) for kv in range(kv_local)], axis=1
        ).astype(jnp.bfloat16)
        scores[at, :] = lax.dot_general(
            spread, kc[row], (((1,), (1,)), ((), ())), preferred_element_type=jnp.float32
        )

    old = jnp.where(mask[...] > 0.0, scores[...] * inv_root, MASKED_SCORE)
    new = score_new[:, :1]
    highest = jnp.maximum(jnp.max(old, axis=-1, keepdims=True), new)
    weight_old = jnp.exp(old - highest)
    weight_new = jnp.exp(new - highest)
    denominator = jnp.sum(weight_old, axis=-1, keepdims=True) + weight_new
    scores[...] = weight_old / denominator
    weight_new = (weight_new / denominator).astype(jnp.bfloat16).astype(jnp.float32)
    values_new[...] = values_new[...] * weight_new

    loads["vc"].wait()
    for row in range(rows):
        at = slice(row * slot, (row + 1) * slot)
        mixed = jnp.dot(
            scores[at, :].astype(jnp.bfloat16), vc[row], preferred_element_type=jnp.float32
        )
        taken = mixed[:, :HEAD_DIM]
        for kv in range(1, kv_local):
            taken = jnp.where(head_of == kv, mixed[:, kv * HEAD_DIM : (kv + 1) * HEAD_DIM], taken)
        attended[at, :] = taken + values_new[at, :]

    flat = jnp.concatenate(
        [
            attended[pl.ds(head, rows, stride=slot), :].astype(jnp.bfloat16)
            for head in range(heads)
        ],
        axis=1,
    )

    loads["wo"].wait()

    def project(half, at):
        start = (2 * at + half) * width
        columns = pl.ds(pl.multiple_of(start, width), width)
        return jnp.dot(flat, wo[:, columns], preferred_element_type=jnp.float32)

    def send_part(at):
        return remote(
            part.at[at], part_in.at[at], part_send.at[at], part_recv.at[at], sibling
        )

    def send_piece(at):
        return remote(
            chip_sum.at[at], piece_in.at[chip], piece_send.at[at], piece_recv.at[chip],
            {"tensor": 2 * at + core},
        )

    for at in range(chips):
        part[at] = project(1 - core, at).astype(jnp.bfloat16)
        send_part(at).start()
    for at in range(chips):
        own = project(core, at)
        send_part(at).wait_recv()
        chip_sum[at] = (own + part_in[at].astype(jnp.float32)).astype(jnp.bfloat16)

        @pl.when(section < sections - 1)
        def _():
            for target in range(chips):
                send_sum(target, at).start()

        @pl.when(chip != at)
        def _():
            send_piece(at).start()

    piece_in[chip] = chip_sum[chip]
    total = jnp.zeros((rows, width), jnp.float32)
    for source in range(chips):
        @pl.when(chip != source)
        def _():
            remote(
                piece_in.at[source], piece_in.at[source], piece_send.at[source],
                piece_recv.at[source], sibling,
            ).wait_recv()

        total = total + piece_in[source].astype(jnp.float32)
    wide = hid[core, chip].astype(jnp.float32)
    out_hidden[0] = (wide + running[0, :, :1] * total).astype(jnp.bfloat16)

    @pl.when(section > 0)
    def _():
        for at in range(chips):
            swap_half(core, at).wait_send()

    @pl.when(section < sections - 1)
    def _():
        send_before().wait_send()
        for at in range(chips):
            for target in range(chips):
                send_sum(target, at).wait_send()

    for at in range(chips):
        send_part(at).wait_send()

        @pl.when(chip != at)
        def _():
            send_piece(at).wait_send()


def solution(mesh):
    sections = mesh.shape["section"]
    tensors = mesh.shape["tensor"]
    chips = tensors // 2

    def per_device(
        inputs, gains, w_query, w_key, w_value, w_out, key_cache, value_cache, cache_lens, exit_plan
    ):
        rows, width = inputs.shape
        features = gains.shape[1]
        query_width = w_query.shape[2]
        kv_width = w_key.shape[2]
        heads = query_width // HEAD_DIM
        groups_per_kv = query_width // kv_width
        slot = -(-heads // 8) * 8
        slots = key_cache.shape[2]
        any_spec = pl.BlockSpec(memory_space=pl.ANY)
        smem_spec = pl.BlockSpec(memory_space=pltpu.SMEM)
        vmem_spec = pl.BlockSpec(memory_space=pltpu.VMEM)
        bf16, f32 = jnp.bfloat16, jnp.float32
        return pl.pallas_call(
            functools.partial(relay_kernel, sections, tensors, groups_per_kv),
            out_shape=(
                jax.ShapeDtypeStruct((1, rows, width), bf16),
                jax.ShapeDtypeStruct((1, rows, kv_width), bf16),
                jax.ShapeDtypeStruct((1, rows, kv_width), bf16),
            ),
            in_specs=[smem_spec] * 2 + [any_spec] * 8,
            out_specs=(vmem_spec,) * 3,
            scratch_shapes=[
                pltpu.VMEM((features, query_width), bf16),
                pltpu.VMEM((features, kv_width), bf16),
                pltpu.VMEM((features, kv_width), bf16),
                pltpu.VMEM((query_width, features), bf16),
                pltpu.VMEM((rows, slots, kv_width), bf16),
                pltpu.VMEM((rows, slots, kv_width), bf16),
                pltpu.VMEM((1, features), f32),
                pltpu.VMEM((2, chips, rows, width), bf16),
                pltpu.VMEM((chips, rows, width), bf16),
                pltpu.VMEM((chips, rows, width), bf16),
                pltpu.VMEM((chips, rows, width), bf16),
                pltpu.VMEM((chips, rows, width), bf16),
                pltpu.VMEM((chips, chips, rows, width), bf16),
                pltpu.VMEM((chips, rows, width), bf16),
                pltpu.VMEM((rows, features), bf16),
                pltpu.VMEM((rows, HEAD_DIM), f32),
                pltpu.VMEM((2, rows, HEAD_DIM), f32),
                pltpu.VMEM((rows * slot, slots), f32),
                pltpu.VMEM((rows * slot, HEAD_DIM), f32),
                pltpu.VMEM((rows * slot, slots), f32),
                pltpu.VMEM((rows * slot, HEAD_DIM), f32),
                pltpu.VMEM((rows * slot, HEAD_DIM), f32),
                pltpu.VMEM((rows * slot, HEAD_DIM), f32),
                pltpu.SemaphoreType.DMA((8,)),
                pltpu.SemaphoreType.DMA((tensors,)),
                pltpu.SemaphoreType.DMA((2, chips)),
                pltpu.SemaphoreType.DMA((chips,)),
                pltpu.SemaphoreType.DMA((chips,)),
                pltpu.SemaphoreType.DMA((1,)),
                pltpu.SemaphoreType.DMA((1,)),
                pltpu.SemaphoreType.DMA((chips,)),
                pltpu.SemaphoreType.DMA((chips,)),
                pltpu.SemaphoreType.DMA((chips, chips)),
                pltpu.SemaphoreType.DMA((chips, chips)),
                pltpu.SemaphoreType.DMA((chips,)),
                pltpu.SemaphoreType.DMA((chips,)),
            ],
            compiler_params=pltpu.CompilerParams(
                collective_id=0, has_side_effects=True, vmem_limit_bytes=63 * 1024 * 1024
            ),
            name="relay",
        )(
            cache_lens, exit_plan, inputs, gains, w_query, w_key, w_value, w_out,
            key_cache, value_cache,
        )

    return jax.shard_map(
        per_device,
        mesh=mesh,
        in_specs=(
            P("group", "tensor"),
            P("section", None),
            P("section", None, "tensor"),
            P("section", None, "tensor"),
            P("section", None, "tensor"),
            P("section", "tensor", None),
            P("section", "group", None, "tensor"),
            P("section", "group", None, "tensor"),
            P("group"),
            P("group"),
        ),
        out_specs=(
            P("section", "group", "tensor"),
            P("section", "group", "tensor"),
            P("section", "group", "tensor"),
        ),
        check_vma=False,
    )
```
